128 devices in a mesh: dp: 16 (over z, y), expert: 8 (over x, core).
Axes of the slice: x: 4, y: 4, z: 4, core: 2. Of those that a mesh axis runs over, the one named last changes fastest.
Arguments:
- hidden: bfloat16 [8, 1024, 8192], P('expert', None, 'dp'), may hold values from -6 to 6
- down_weight: bfloat16 [8, 8192, 6144], P('expert', 'dp'), may hold values from -0.0625 to 0.0625
- grad_out: bfloat16 [2048, 6144], P('dp', 'expert'), may hold values from -2 to 2
- routing: int32 [2048, 2], P('dp'), may hold values from 0 to 7, all different within a row; in each aligned block of 128 rows (0 to 127, 128 to 255, ...) at most 64 rows name the same one
- gates: float32 [2048, 2], P('dp'), may hold values from 0.25 to 1
Outputs:
- mixed_out: bfloat16 [2048, 6144], P('dp', 'expert')
- grad_hidden: bfloat16 [8, 1024, 8192], P('expert', None, 'dp')
- grad_weight: bfloat16 [8, 8192, 6144], P('expert', 'dp')
The draws below stay inside these ranges and needn't reach their ends.
Inputs may be any that keep to these rules, and one draw needn't show every extreme that they name: `routing`: among the 128 tokens of one sequence shard (aligned blocks of rows), each expert is named by at most 64 tokens, a bound that some block reaches; a token names 2 different experts.
All inputs are finite; a program needn't handle non-finite values.
Results may differ from the reference program's by a relative error of at most 0.017.
Values may be sent and summed in bfloat16 or wider, within the bound.
A program may use at most 128 MiB of HBM per device.

```python
import math
import jax
import jax.numpy as jnp
import numpy as np
from jax import lax

D = 6144
TOP = 2
HID = 8192
TOK_DEV = 128
EXPERTS = 8
CAP = 64
SLOTS = 1024
TOKENS = 2048
N_DP = 16


def with_spikes(array, rng, source, target, blocks, factor):
    owner, partner = [(jnp.arange(array.shape[axis_at]) // (array.shape[axis_at] // blocks)).reshape([-1 if axis == axis_at else 1 for axis in range(array.ndim)]) for axis_at in (source, target)]
    chosen = jax.random.permutation(rng, blocks)[partner]
    strong = (owner == chosen) | (owner == (partner + blocks // 2) % blocks)
    return jnp.where(strong, factor * array, array)


def steps_of(rng, shape, split, least, largest):
    loudness, own = 1.0, jax.random.fold_in(rng, 6)
    for dim, blocks in split:
        draws = jnp.exp(jax.random.uniform(jax.random.fold_in(own, dim), (blocks,), jnp.float32, least / len(split), largest / len(split)))
        loudness = loudness * jnp.repeat(draws, shape[dim] // blocks).reshape([-1 if axis == dim else 1 for axis in range(len(shape))])
    return loudness


def shared_out(own_key, own, number, rows, number_of, top, reach, lean):
    order = jax.random.permutation(own_key, number_of)
    crowded, common = shares(number_of, rows * top, reach, lean, True), shares(number_of, rows * top, reach, lean, False)
    places = jnp.arange(number_of)

    def named(sizes, offset_by):
        used = int((sizes > 0).sum())
        fixed = max(1, used // 4)
        shifted = fixed + (places - fixed + offset_by * (used - fixed)) % max(1, number_of - fixed)
        return jnp.zeros((number_of,), jnp.int32).at[order[jnp.where(places < fixed, places, shifted)]].set(jnp.asarray(sizes, jnp.int32))

    sizes = jnp.where(number % 4 == 0, named(crowded, number // 4), named(common, number - number // 4 - 1))
    mixed = jax.random.permutation(jax.random.fold_in(own, 3), number_of)
    giver, sink = mixed[0:number_of // 2 * 2:2], mixed[1:number_of // 2 * 2:2]
    room = jnp.minimum(sizes[giver] - 1, reach - sizes[sink]) // 2
    room = jnp.where((giver == order[0]) | (sink == order[0]) | (sizes[sink] == 0), 0, jnp.maximum(room, 0))
    shifted = jax.random.randint(jax.random.fold_in(own, 4), (number_of // 2,), 0, 1 << 20) % (room + 1)
    sizes = sizes.at[giver].add(-shifted).at[sink].add(shifted)
    members = jnp.searchsorted(jnp.cumsum(sizes), jnp.arange(rows * top), side="right").astype(jnp.int32)
    table = members.reshape(top, rows).T
    table = table[jax.random.permutation(jax.random.fold_in(own, 1), rows)]
    offset_by = jax.random.randint(jax.random.fold_in(own, 2), (rows, 1), 0, top)
    return jnp.take_along_axis(table, (jnp.arange(top)[None, :] + offset_by) % top, axis=1)


def shares(amount, total, limit, skew, full):
    weights = [(1 << 20) // math.isqrt(grade ** skew) + 1 for grade in range(1, amount + 1)]
    largest = limit if full else min(limit, max(-(-total // amount), total * weights[0] // sum(weights)))
    least = 1 if total - largest >= amount - 1 else 0
    counts, spare = [largest] + [least] * (amount - 1), total - largest - least * (amount - 1)
    while spare > 0:
        free = [i for i in range(1, amount) if counts[i] < largest] or [i for i in range(1, amount) if counts[i] < limit]
        pool, budget = sum([weights[i] for i in free]), spare
        for i in free:
            addition = min(limit - counts[i], max(1, budget * weights[i] // pool), spare)
            counts[i] = counts[i] + addition
            spare = spare - addition
    return np.array(counts)


def scatter_about(stream_key, shape, deviation, limit, cuts=(), kind=jnp.bfloat16):
    result = deviation * jax.random.normal(stream_key, shape, jnp.float32)
    if cuts:
        result = result * steps_of(stream_key, shape, cuts, -0.22, 0.18)
    return jnp.clip(result, -limit, limit).astype(kind)


def bell_draw_with(rng, extent, deviation, most, cuts, heavy, kind=jnp.bfloat16):
    array = deviation * jax.random.normal(rng, extent, jnp.float32)
    if cuts:
        array = array * steps_of(rng, extent, cuts, -0.22, 0.18)
    return jnp.clip(with_spikes(array, jax.random.fold_in(rng, 3), *heavy), -most, most).astype(kind)


def setup_inputs(seed: int = 0) -> dict:
    splits = jax.random.split(jax.random.key(seed), 6)
    hidden = bell_draw_with(splits[0], (EXPERTS, SLOTS, HID), 1.0, 6.0, ((0, 8), (2, 16)), (2, 1, 16, 2.0))
    down_weight = scatter_about(splits[1], (EXPERTS, HID, D), HID ** -0.5, 0.0625, ((0, 8), (1, 16)))
    grad_out = scatter_about(splits[2], (TOKENS, D), 0.3, 2.0, ((0, 16), (1, 8)))
    routing_keys = jax.random.split(jax.random.fold_in(splits[3], 1), TOKENS // TOK_DEV)
    routing_turns = jax.random.permutation(jax.random.fold_in(splits[3], 3), TOKENS // TOK_DEV)
    routing = jax.vmap(lambda own, number: shared_out(jax.random.fold_in(splits[3], 2), own, number, TOK_DEV, EXPERTS, TOP, CAP, 2))(routing_keys, routing_turns).reshape((TOKENS, TOP))
    gates = jnp.clip(0.25 + 0.75 * jax.random.uniform(splits[4], (TOKENS, TOP), jnp.float32) ** steps_of(splits[4], (TOKENS, TOP), ((0, 16),), -0.2, 0.2), 0.25, 1.0)
    return dict(hidden=hidden, down_weight=down_weight, grad_out=grad_out, routing=routing, gates=gates)


def dispatch_weights(routing, gates, experts, capacity):
    flattened = routing.reshape(-1).astype(jnp.int32)
    onehot = (flattened[:, None] == jnp.arange(experts, dtype=jnp.int32)[None, :]).astype(jnp.int32)
    position = jnp.sum((jnp.cumsum(onehot, axis=0) - onehot) * onehot, axis=1)
    target = flattened * capacity + position
    picked = (jnp.arange(experts * capacity, dtype=jnp.int32)[:, None] == target[None, :]).astype(jnp.float32)
    picked = picked * gates.reshape(-1)[None, :].astype(jnp.float32)
    return jnp.sum(picked.reshape(experts * capacity, routing.shape[0], routing.shape[1]), axis=2)


def shard_dispatch(shard_routes, shard_gates):
    return dispatch_weights(shard_routes, shard_gates, EXPERTS, CAP)


def reference(hidden, down_weight, grad_out, routing, gates):
    highest = lax.Precision.HIGHEST
    width = HID // N_DP
    dispatch = jax.vmap(shard_dispatch)(routing.reshape(N_DP, TOK_DEV, TOP), gates.reshape(N_DP, TOK_DEV, TOP))
    expert_outs = []
    for expert_id in range(EXPERTS):
        total = jnp.zeros((SLOTS, D), jnp.float32)
        for block_id in range(N_DP):
            lower = block_id * width
            part = jnp.dot(hidden[expert_id, :, lower:lower + width], down_weight[expert_id, lower:lower + width, :], preferred_element_type=jnp.float32)
            rounded = lax.optimization_barrier(part.astype(jnp.bfloat16))
            total = total + rounded.astype(jnp.float32)
        expert_outs.append(total.astype(jnp.bfloat16))
    stacked = jnp.stack(expert_outs).reshape(EXPERTS, N_DP, CAP, D).transpose(1, 0, 2, 3)
    stacked = stacked.reshape(N_DP, EXPERTS * CAP, D).astype(jnp.float32)
    mixed_out = jnp.einsum("dst,dsf->dtf", dispatch, stacked, precision=highest)
    mixed_out = mixed_out.reshape(TOKENS, D).astype(jnp.bfloat16)
    grads = grad_out.reshape(N_DP, TOK_DEV, D).astype(jnp.float32)
    routed = jnp.einsum("dst,dtf->dsf", dispatch, grads, precision=highest).astype(jnp.bfloat16)
    routed = routed.reshape(N_DP, EXPERTS, CAP, D).transpose(1, 0, 2, 3).reshape(EXPERTS, SLOTS, D)
    grad_hidden = []
    grad_weight = []
    for expert_id in range(EXPERTS):
        grad_hidden.append(jnp.dot(routed[expert_id], down_weight[expert_id].T, preferred_element_type=jnp.float32).astype(jnp.bfloat16))
        grad_weight.append(jnp.dot(hidden[expert_id].T, routed[expert_id], preferred_element_type=jnp.float32).astype(jnp.bfloat16))
    return (mixed_out, jnp.stack(grad_hidden), jnp.stack(grad_weight))
```

```python
import jax
import jax.numpy as jnp
from jax import lax
from jax.experimental import pallas as pl
from jax.experimental.pallas import tpu as pltpu
from jax.sharding import PartitionSpec as P

AXES = (("x", "y", "z"), ("y", "z", "x"), ("z", "x", "y"))
MESH = pl.DeviceIdType.MESH
BF16 = jnp.bfloat16
F32 = jnp.float32
DN_T = (((1,), (1,)), ((), ()))


def dot(a, b):
    return jnp.dot(a, b, preferred_element_type=F32)


def kernel(
    hid, w, gin, rt, gt,
    mixed, ghid, gwt,
    go, ps, ra1, rb1, fl1, fr1, ra2, rb2, fl2, fr2, ra3, rb3, fl3, fr3,
    wv, hv, ht, mv, rv, acc, gws, ghr, gm, info, mst,
    ag_s, ag_r, rs_s, rs_r, w_s, w_r, h_s, h_r, in_s, in_r, gw_s, gw_r, gh_s, gh_r,
    wl, hl, gl, gwl, outl,
):
    dp = lax.axis_index("dp")
    ex = lax.axis_index("expert")
    z, y = lax.div(dp, 4), lax.rem(dp, 4)
    x, c = lax.div(ex, 2), lax.rem(ex, 2)
    oc = 1 - c
    co = {"x": x, "y": y, "z": z}
    ras, rbs, fls, frs = (ra1, ra2, ra3), (rb1, rb2, rb3), (fl1, fl2, fl3), (fr1, fr2, fr3)

    def at(axis, delta):
        return lax.rem(co[axis] + (delta + 4), 4)

    def near(axis, delta):
        q = dict(co)
        q[axis] = at(axis, delta)
        return (q["z"] * 4 + q["y"], q["x"] * 2 + c)

    partner = (dp, x * 2 + oc)

    def remote(src, dst, ssem, rsem, device):
        return pltpu.make_async_remote_copy(
            src_ref=src, dst_ref=dst, send_sem=ssem, recv_sem=rsem, device_id=device, device_id_type=MESH
        )

    row = lax.broadcasted_iota(jnp.int32, (8, 128), 0)
    eid = x * 2 + lax.rem(row, 2)
    is0 = rt[0:1, :] == eid
    is1 = rt[1:2, :] == eid
    gate = jnp.where(is0, gt[0:1, :], 0.0) + jnp.where(is1, gt[1:2, :], 0.0)
    named = jnp.where(is0, 1.0, 0.0) + jnp.where(is1, 1.0, 0.0)
    before = jnp.where(
        lax.broadcasted_iota(jnp.int32, (128, 128), 0) < lax.broadcasted_iota(jnp.int32, (128, 128), 1), 1.0, 0.0
    )
    rank = dot(jnp.concatenate([named, named], axis=0).astype(BF16), before.astype(BF16))[0:8, :]
    info[dp] = jnp.where(row < 2, jnp.where(named > 0.5, rank, -1.0), gate)

    barrier = pltpu.get_barrier_semaphore()

    def greet(k, carry):
        pl.semaphore_signal(barrier, inc=1, device_id=(lax.rem(dp + k, 16), ex), device_id_type=MESH)
        return carry

    lax.fori_loop(1, 16, greet, 0)
    for device in (near("x", 1), near("x", -1), partner):
        pl.semaphore_signal(barrier, inc=1, device_id=device, device_id_type=MESH)
    pl.semaphore_wait(barrier, 18)

    def slab(k, p, j, h):
        i1, i2 = co[AXES[p][0]], co[AXES[p][1]]
        if k == 0:
            return go.at[p, i1, i2, j, pl.ds(64 * h, 64)]
        if k == 1:
            return go.at[p, i1, j, pl.ds(2 * h, 2)]
        return go.at[p, j, pl.ds(2 * h, 2)]

    def ag_copy(k, p, n, receive):
        axis = AXES[p][2 - k]
        own, left, right, far = at(axis, 0), at(axis, -1), at(axis, 1), at(axis, 2)
        h = (0, 1, 1, 0, 0, 1)[n]
        j = ((left, right, left, right, far, far) if receive else (own, own, own, own, left, right))[n]
        dst = slab(k, p, j, h)
        src = dst
        if k == 0 and n < 4 and not receive:
            src = gin.at[pl.ds(64 * h, 64), pl.ds(256 * p, 256)]
        device = near(axis, (1, -1, 1, -1, 1, -1)[n])
        return remote(src, dst, ag_s.at[p, k, n], ag_r.at[p, k, n], device)

    def ag_start(k, p):
        for n in range(4):
            ag_copy(k, p, n, False).start()

    def ag_relay(k, p):
        for n in range(2):
            ag_copy(k, p, n, True).wait_recv()
            ag_copy(k, p, n + 4, False).start()

    def ag_finish(k, p):
        for n in range(2, 6):
            ag_copy(k, p, n, True).wait_recv()

    def chunk(k, p, j, h):
        i1, i2 = co[AXES[p][0]], co[AXES[p][1]]
        if k == 0:
            return ps.at[p, j, pl.ds(2 * h, 2)]
        if k == 1:
            return ps.at[p, i1, j, pl.ds(2 * h, 2)]
        return ps.at[p, i1, i2, j, pl.ds(64 * h, 64)]

    def half(ref, k, p, h):
        return ref.at[p, pl.ds(2 * h, 2)] if k < 2 else ref.at[p, pl.ds(64 * h, 64)]

    def rs_copy(k, p, n):
        axis = AXES[p][k]
        h = (0, 1, 1, 0, 0, 1)[n]
        j = at(axis, (2, 2, 1, -1, 1, -1)[n])
        if n == 0:
            dst = ras[k].at[p]
        elif n == 1:
            dst = rbs[k].at[p]
        else:
            dst = half((fls, frs)[n % 2][k] if n > 3 else (fls, frs)[n - 2][k], k, p, h)
        device = near(axis, (1, -1, 1, -1, 1, -1)[n])
        return remote(chunk(k, p, j, h), dst, rs_s.at[p, k, n], rs_r.at[p, k, n], device)

    def add_into(dst, sources, k):
        if k == 2:
            total = dst[...].astype(F32)
            for source in sources:
                total = total + source[...].astype(F32)
            dst[...] = total.astype(BF16)
            return
        count = dst.shape[0]
        if k == 0:
            def one(n, carry):
                a, b = lax.div(n, 4), lax.rem(n, 4)
                total = dst[a, b].astype(F32)
                for source in sources:
                    total = total + source[a, b].astype(F32)
                dst[a, b] = total.astype(BF16)
                return carry

            lax.fori_loop(0, count * 4, one, 0)
        else:
            def one(n, carry):
                total = dst[n].astype(F32)
                for source in sources:
                    total = total + source[n].astype(F32)
                dst[n] = total.astype(BF16)
                return carry

            lax.fori_loop(0, count, one, 0)

    def rs_relay(k, p):
        axis = AXES[p][k]
        rs_copy(k, p, 0).wait_recv()
        add_into(chunk(k, p, at(axis, 1), 0), (ras[k].at[p],), k)
        rs_copy(k, p, 4).start()
        rs_copy(k, p, 1).wait_recv()
        add_into(chunk(k, p, at(axis, -1), 1), (rbs[k].at[p],), k)
        rs_copy(k, p, 5).start()

    def rs_finish(k, p):
        for n in range(2, 6):
            rs_copy(k, p, n).wait_recv()
        i1, i2, i3 = (co[axis] for axis in AXES[p])
        if k == 0:
            add_into(ps.at[p, i1], (fls[k].at[p], frs[k].at[p]), k)
        elif k == 1:
            add_into(ps.at[p, i1, i2], (fls[k].at[p], frs[k].at[p]), k)
        else:
            total = ps[p, i1, i2, i3].astype(F32) + fls[k][p].astype(F32) + frs[k][p].astype(F32)
            mst[:, 256 * p:256 * (p + 1)] = total.astype(BF16)

    for p in range(3):
        ag_start(0, p)

    def info_copy(k, receive):
        place = lax.rem(dp + 16 - k, 16) if receive else dp
        return remote(info.at[dp], info.at[place], in_s.at[k], in_r.at[k], (lax.rem(dp + k, 16), ex))

    def info_start(k, carry):
        info_copy(k, False).start()
        return carry

    lax.fori_loop(1, 16, info_start, 0)

    def h_copy(e, device):
        return remote(hid, hv.at[:, pl.ds(pl.multiple_of(e * 64, 64), 64), :], h_s, h_r, device)

    def w_copy(b, e, of, device):
        cols = pl.ds(pl.multiple_of(b * 1536 + of * 768, 128), 768)
        rows = pl.ds(pl.multiple_of(e * 512, 512), 512)
        return remote(w.at[:, cols], wv.at[rows, pl.ds(b * 768, 768)], w_s.at[b], w_r.at[b], device)

    def w_local(b):
        cols = pl.ds(pl.multiple_of(b * 1536 + c * 768, 128), 768)
        rows = pl.ds(pl.multiple_of(c * 512, 512), 512)
        return pltpu.make_async_copy(w.at[:, cols], wv.at[rows, pl.ds(b * 768, 768)], wl.at[b])

    h_copy(c, partner).start()
    for b in range(4):
        w_copy(b, c, oc, partner).start()
    h_local = pltpu.make_async_copy(hid, hv.at[:, pl.ds(pl.multiple_of(c * 64, 64), 64), :], hl)
    h_local.start()

    def g_local(p):
        i1, i2, i3 = (co[axis] for axis in AXES[p])
        return pltpu.make_async_copy(gin.at[:, pl.ds(256 * p, 256)], go.at[p, i1, i2, i3], gl.at[p])

    for p in range(3):
        g_local(p).start()
    for b in range(4):
        w_local(b).start()

    for p in range(3):
        ag_relay(0, p)
    for p in range(3):
        g_local(p).wait()
        ag_finish(0, p)
        ag_start(1, p)
    for p in range(3):
        ag_relay(1, p)
    for p in range(3):
        ag_finish(1, p)
        ag_start(2, p)

    h_local.wait()
    h_copy(oc, partner).wait_recv()

    def info_wait(k, carry):
        info_copy(k, True).wait_recv()
        return carry

    lax.fori_loop(1, 16, info_wait, 0)
    slot = lax.broadcasted_iota(jnp.int32, (128, 128), 0).astype(F32)
    lane = lax.broadcasted_iota(jnp.int32, (128, 128), 1)

    def mix(d, carry):
        part = info[d]
        first = jnp.where(part[0:1, :] == slot, part[2:3, :], 0.0)
        second = jnp.where(part[1:2, :] == slot - 64.0, part[3:4, :], 0.0)
        spread = first + second
        gm[d] = spread.astype(BF16)
        turned = spread.T
        rows = hv[d]
        zz, yy = lax.div(d, 4), lax.rem(d, 4)
        mv[zz, yy, :, 0:512] = dot(jnp.where(lane < 64, turned, 0.0).astype(BF16), rows).astype(BF16)
        mv[zz, yy, :, 512:1024] = dot(jnp.where(lane < 64, 0.0, turned).astype(BF16), rows).astype(BF16)
        return carry

    lax.fori_loop(0, 16, mix, 0)

    for b in range(4):
        w_local(b).wait()
        w_copy(b, oc, c, partner).wait_recv()

    def forward(p, k):
        def tile(n, carry):
            if p == 0:
                left = mv[n]
                cols = k * 768
            elif p == 1:
                left = mv[:, k]
                cols = n * 768 + 256
            else:
                left = mv[k]
                cols = n * 768 + 512
            right = wv[:, pl.ds(pl.multiple_of(cols, 128), 256)]
            out = dot(left.reshape(512, 1024), right).astype(BF16).reshape(4, 128, 256)
            if p < 2:
                ps[p, k, :, n] = out
            else:
                ps[p, k, n] = out
            return carry

        lax.fori_loop(0, 4, tile, 0)

    for p in range(3):
        forward(p, at(AXES[p][0], 2))
        rs_copy(0, p, 0).start()
        rs_copy(0, p, 1).start()
        ag_relay(2, p)
    for p in range(3):
        forward(p, at(AXES[p][0], 1))
        rs_copy(0, p, 2).start()
        forward(p, at(AXES[p][0], -1))
        rs_copy(0, p, 3).start()
    for p in range(3):
        forward(p, at(AXES[p][0], 0))

    for e in range(2):
        def turn(n, carry, e=e):
            pair = jnp.concatenate([hv[n * 2, e * 64:e * 64 + 64, :], hv[n * 2 + 1, e * 64:e * 64 + 64, :]], axis=0)
            ht[e, :, pl.ds(pl.multiple_of(n * 128, 128), 128)] = pair.T
            return carry

        lax.fori_loop(0, 8, turn, 0)

    for p in range(3):
        ag_finish(2, p)

    def gw_out(b, mine):
        e = c if mine else oc
        cols = pl.ds(pl.multiple_of(b * 1536 + c * 768, 128), 768)
        if mine:
            return pltpu.make_async_copy(gws.at[e], gwt.at[:, cols], gwl.at[b])
        return remote(gws.at[e], gwt.at[:, cols], gw_s.at[b], gw_r.at[b], partner)

    def gw_in(b):
        cols = pl.ds(pl.multiple_of(b * 1536 + oc * 768, 128), 768)
        return remote(gws.at[c], gwt.at[:, cols], gw_s.at[b], gw_r.at[b], partner)

    def routed(b):
        def one(d, carry):
            zz, yy = lax.div(d, 4), lax.rem(d, 4)
            left = gm[d]
            start = pl.multiple_of(d * 64, 64)
            for p, right in enumerate((go[0, b, yy, zz], go[1, yy, zz, b], go[2, zz, b, yy])):
                out = dot(left, right).astype(BF16)
                rv[0, pl.ds(start, 64), 256 * p:256 * (p + 1)] = out[0:64]
                rv[1, pl.ds(start, 64), 256 * p:256 * (p + 1)] = out[64:128]
            return carry

        lax.fori_loop(0, 16, one, 0)

    def weight_grad(b, e):
        def one(n, carry):
            cols = pl.ds(pl.multiple_of(n * 256, 256), 256)
            gws[e, :, cols] = dot(ht[e], rv[e, :, cols]).astype(BF16)
            return carry

        lax.fori_loop(0, 3, one, 0)

    def hidden_grad(b, e):
        def one(n, carry):
            rows = pl.ds(pl.multiple_of(n * 256, 256), 256)
            right = wv[pl.ds(pl.multiple_of(e * 512, 512), 512), pl.ds(b * 768, 768)]
            out = lax.dot_general(rv[e, rows, :], right, DN_T, preferred_element_type=F32)
            acc[e, rows, :] = out if b == 0 else acc[e, rows, :] + out
            return carry

        lax.fori_loop(0, 4, one, 0)

    def backward(b):
        routed(b)
        if b:
            gw_out(b - 1, False).wait_send()
        weight_grad(b, oc)
        gw_out(b, False).start()
        hidden_grad(b, oc)
        if b:
            gw_out(b - 1, True).wait()
        weight_grad(b, c)
        gw_out(b, True).start()
        hidden_grad(b, c)

    backward(0)
    for p in range(3):
        rs_relay(0, p)
    backward(1)
    backward(2)
    backward(3)

    gh_copy = remote(hv.at[:, 0:64, :], ghr, gh_s, gh_r, partner)

    def pack(d, carry):
        hv[d, 0:64, :] = acc[oc, pl.ds(pl.multiple_of(d * 64, 64), 64), :].astype(BF16)
        return carry

    lax.fori_loop(0, 16, pack, 0)
    gh_copy.start()
    for p in range(3):
        rs_finish(0, p)
        for n in range(4):
            rs_copy(1, p, n).start()
    gh_copy.wait_recv()

    def close(d, carry):
        own = acc[c, pl.ds(pl.multiple_of(d * 64, 64), 64), :]
        hv[d, 64:128, :] = (own + ghr[d].astype(F32)).astype(BF16)
        return carry

    lax.fori_loop(0, 16, close, 0)
    gh_out = pltpu.make_async_copy(hv.at[:, 64:128, :], ghid, outl.at[0])
    gh_out.start()
    for p in range(3):
        rs_relay(1, p)
    for p in range(3):
        rs_finish(1, p)
        for n in range(4):
            rs_copy(2, p, n).start()
    for p in range(3):
        rs_relay(2, p)
    for p in range(3):
        rs_finish(2, p)
    mixed_out = pltpu.make_async_copy(mst, mixed, outl.at[1])
    mixed_out.start()

    for p in range(3):
        for k in range(3):
            for n in range(6):
                ag_copy(k, p, n, False).wait_send()
                rs_copy(k, p, n).wait_send()

    def info_end(k, carry):
        info_copy(k, False).wait_send()
        return carry

    lax.fori_loop(1, 16, info_end, 0)
    h_copy(c, partner).wait_send()
    for b in range(4):
        w_copy(b, c, oc, partner).wait_send()
        gw_in(b).wait_recv()
    gw_out(3, False).wait_send()
    gw_out(3, True).wait()
    gh_copy.wait_send()
    gh_out.wait()
    mixed_out.wait()


def body(hidden, down_weight, grad_out, routing, gates):
    dma = pltpu.SemaphoreType.DMA
    sums = []
    for lead, rows in (((2, 4), 128), ((2,), 128), ((), 64)):
        whole = {2: (4, 4, 128, 256), 1: (4, 128, 256), 0: (128, 256)}[len(lead)]
        sums += [pltpu.VMEM((3, *lead, rows, 256), BF16)] * 2 + [pltpu.VMEM((3, *whole), BF16)] * 2
    anywhere = pl.BlockSpec(memory_space=pl.ANY)
    inside = pl.BlockSpec(memory_space=pltpu.VMEM)
    mixed, ghid, gwt = pl.pallas_call(
        kernel,
        out_shape=(
            jax.ShapeDtypeStruct((128, 768), BF16),
            jax.ShapeDtypeStruct((16, 64, 512), BF16),
            jax.ShapeDtypeStruct((512, 6144), BF16),
        ),
        in_specs=[anywhere, anywhere, anywhere, inside, inside],
        out_specs=(anywhere, anywhere, anywhere),
        scratch_shapes=[
            pltpu.VMEM((3, 4, 4, 4, 128, 256), BF16),
            pltpu.VMEM((3, 4, 4, 4, 128, 256), BF16),
            *sums,
            pltpu.VMEM((1024, 3072), BF16),
            pltpu.VMEM((16, 128, 512), BF16),
            pltpu.VMEM((2, 512, 1024), BF16),
            pltpu.VMEM((4, 4, 128, 1024), BF16),
            pltpu.VMEM((2, 1024, 768), BF16),
            pltpu.VMEM((2, 1024, 512), F32),
            pltpu.VMEM((2, 512, 768), BF16),
            pltpu.VMEM((16, 64, 512), BF16),
            pltpu.VMEM((16, 128, 128), BF16),
            pltpu.VMEM((16, 8, 128), F32),
            pltpu.VMEM((128, 768), BF16),
            dma((3, 3, 6)), dma((3, 3, 6)), dma((3, 3, 6)), dma((3, 3, 6)),
            dma((4,)), dma((4,)), dma(()), dma(()), dma((16,)), dma((16,)),
            dma((4,)), dma((4,)), dma(()), dma(()),
            dma((4,)), dma(()), dma((3,)), dma((4,)), dma((2,)),
        ],
        compiler_params=pltpu.CompilerParams(
            collective_id=0, has_side_effects=True, vmem_limit_bytes=67043328
        ),
    )(
        hidden.reshape(16, 64, 512),
        down_weight[0],
        grad_out,
        routing.T,
        gates.T,
    )
    return mixed, ghid.reshape(1, 1024, 512), gwt[None]


def solution(mesh):
    return jax.shard_map(
        body,
        mesh=mesh,
        in_specs=(
            P("expert", None, "dp"),
            P("expert", "dp", None),
            P("dp", "expert"),
            P("dp", None),
            P("dp", None),
        ),
        out_specs=(P("dp", "expert"), P("expert", None, "dp"), P("expert", "dp", None)),
        check_vma=False,
    )
```

```python
import jax
import jax.numpy as jnp
from jax import lax
from jax.experimental import pallas as pl
from jax.experimental.pallas import tpu as pltpu
from jax.sharding import PartitionSpec as P

AXES = (("x", "y", "z"), ("y", "z", "x"), ("z", "x", "y"))
MESH = pl.DeviceIdType.MESH
BF16 = jnp.bfloat16
F32 = jnp.float32
RATE = 1.4
HOP = 2.0
DN_T = (((1,), (1,)), ((), ()))


def dot(a, b):
    return jnp.dot(a, b, preferred_element_type=F32)


class Clock:
    def __init__(self):
        self.now, self.links, self.pending, self.done, self.count = 0.0, {}, [], set(), 0

    def send(self, copy, size, link):
        copy.start()
        begin = max(self.now, self.links.get(link, 0.0))
        self.links[link] = begin + size / RATE
        return self.links[link] + HOP

    def later(self, ready, needs, act):
        self.count += 1
        self.pending.append((ready, self.count, needs, act))

    def step(self, limit):
        able = [item for item in self.pending if item[0] <= limit and self.done.issuperset(item[2])]
        if not able:
            return False
        item = min(able, key=lambda item: item[:2])
        self.pending.remove(item)
        self.now = max(self.now, item[0])
        item[3]()
        return True

    def flush(self):
        while self.step(self.now):
            pass

    def wait(self, tags):
        while not self.done.issuperset(tags):
            assert self.step(float("inf"))

    def run(self, cost, act, *args):
        self.flush()
        act(*args)
        self.now += cost


def kernel(
    hid, w, gin, rt, gt,
    mixed, ghid, gwt,
    go, ps, ra1, rb1, fl1, fr1, ra2, rb2, fl2, fr2, ra3, rb3, fl3, fr3,
    wv, hv, ht, mv, rv, acc, gws, ghr, gm, info, mst,
    ag_s, ag_r, rs_s, rs_r, w_s, w_r, h_s, h_r, in_s, in_r, gw_s, gw_r, gh_s, gh_r,
    wl, hl, gl, gwl, outl,
):
    dp = lax.axis_index("dp")
    ex = lax.axis_index("expert")
    z, y = lax.div(dp, 4), lax.rem(dp, 4)
    x, c = lax.div(ex, 2), lax.rem(ex, 2)
    oc = 1 - c
    co = {"x": x, "y": y, "z": z}
    clock = Clock()

    def at(axis, delta):
        return lax.rem(co[axis] + delta, 4)

    def rel(axis, place):
        return lax.rem(place + 4 - co[axis], 4)

    def near(axis, delta):
        q = dict(co)
        q[axis] = at(axis, delta % 4)
        return (q["z"] * 4 + q["y"], q["x"] * 2 + c)

    partner = (dp, x * 2 + oc)

    def remote(src, dst, ssem, rsem, device):
        return pltpu.make_async_remote_copy(
            src_ref=src, dst_ref=dst, send_sem=ssem, recv_sem=rsem, device_id=device, device_id_type=MESH
        )

    barrier = pltpu.get_barrier_semaphore()

    for device in [near(axis, side) for axis in "xyz" for side in (1, -1)] + [near("y", 2), near("z", 2), partner]:
        pl.semaphore_signal(barrier, inc=1, device_id=device, device_id_type=MESH)

    row = lax.broadcasted_iota(jnp.int32, (8, 128), 0)
    eid = x * 2 + lax.rem(row, 2)
    is0 = rt[0:1, :] == eid
    is1 = rt[1:2, :] == eid
    gate = jnp.where(is0, gt[0:1, :], 0.0) + jnp.where(is1, gt[1:2, :], 0.0)
    named = jnp.where(is0, 1.0, 0.0) + jnp.where(is1, 1.0, 0.0)
    before = jnp.where(
        lax.broadcasted_iota(jnp.int32, (128, 128), 0) < lax.broadcasted_iota(jnp.int32, (128, 128), 1), 1.0, 0.0
    )
    rank = dot(jnp.concatenate([named, named], axis=0).astype(BF16), before.astype(BF16))[0:8, :]
    info[0, 0] = jnp.where(row < 2, jnp.where(named > 0.5, rank, -1.0), gate)

    def w_local(b):
        cols = pl.ds(pl.multiple_of(b * 1536 + c * 768, 128), 768)
        rows = pl.ds(pl.multiple_of(c * 512, 512), 512)
        return pltpu.make_async_copy(w.at[:, cols], wv.at[rows, pl.ds(b * 768, 768)], wl)

    def g_local(p, h):
        return pltpu.make_async_copy(
            gin.at[pl.ds(64 * h, 64), pl.ds(256 * p, 256)], go.at[p, h, 0, 0, 0], gl
        )

    h_local = pltpu.make_async_copy(hid, hv.at[:, pl.ds(pl.multiple_of(c * 64, 64), 64), :], hl)
    h_local.start()
    for p in range(3):
        for h in range(2):
            g_local(p, h).start()
    for b in range(4):
        w_local(b).start()
    pl.semaphore_wait(barrier, 9)

    def region(ref, p, h, k, g, q):
        one, rest = pl.ds(0, 1), pl.ds(1, 3)
        if k == 2:
            return ref.at[p, h, 0, 0, pl.ds(q, 1) if isinstance(q, int) else q]
        if k == 1:
            return ref.at[p, h, 0, q, rest if g & 1 else one]
        return ref.at[p, h, q, rest if g & 2 else one, rest if g & 1 else one]

    BLOCKS = (1, 3, 3, 9)
    SIDES = (1, -1, 1, -1, 1, -1)
    HALVES = (0, 1, 1, 0, 0, 1)

    def slot(k, g):
        return (0, 4, 6)[k] + g

    def ag_copy(k, p, g, n):
        axis, h = AXES[p][k], HALVES[n]
        q = (3, 1, 3, 1, 2, 2)[n]
        dst = region(go, p, h, k, g, q)
        src = region(go, p, h, k, g, (0, 0, 0, 0, 3, 1)[n])
        s = slot(k, g)
        return remote(src, dst, ag_s.at[k], ag_r.at[p, s, min(n // 2, 1)], near(axis, SIDES[n]))

    def ag_send(k, p, g, n):
        return clock.send(ag_copy(k, p, g, n), BLOCKS[g], (AXES[p][k], SIDES[n]))

    def taken(ref, k, p, g, late):
        some = region(go, p, pl.ds(0, 2), k, g, pl.ds(1, 2) if late else pl.ds(1, 1))
        remote(some, some, ref, ref, partner).wait_recv()

    def ag_start(k, p, g):
        due = [ag_send(k, p, g, n) for n in range(4)]

        def relay():
            taken(ag_r.at[p, slot(k, g), 0], k, p, g, False)
            last = [ag_send(k, p, g, n) for n in (4, 5)]
            clock.done.add(("passed", k, p, g))
            clock.later(max(due + last), (), finish)

        def finish():
            taken(ag_r.at[p, slot(k, g), 1], k, p, g, True)
            clock.done.add(("ag", k, p, g))
            if (k, g) == (2, 0):
                ag_start(1, p, 1)
                ag_start(0, p, 1)
            elif k == 1:
                ag_start(0, p, 2 + g)

        clock.later(max(due[:2]), (), relay)

    def rs_place(k, p, g, n):
        one, rest = pl.ds(0, 1), pl.ds(1, 3)
        a, b = (rest if g & 2 else one), (rest if g & 1 else one)
        if n < 2:
            ref = ((ra1, ra2, ra3), (rb1, rb2, rb3))[n][k].at[p]
        else:
            ref = ((fl1, fl2, fl3), (fr1, fr2, fr3))[n % 2][k].at[p, HALVES[n]]
        return ref.at[a, b] if k == 0 else ref.at[b] if k == 1 else ref

    def rs_copy(k, p, g, n):
        src = region(ps, p, HALVES[n], k, g, (2, 2, 1, 3, 1, 3)[n])
        s = slot(k, g)
        return remote(src, rs_place(k, p, g, n), rs_s.at[k], rs_r.at[p, s, min(n // 2, 1)], near(AXES[p][k], SIDES[n]))

    def rs_send(k, p, g, n):
        return clock.send(rs_copy(k, p, g, n), BLOCKS[g], (AXES[p][k], SIDES[n]))

    def add_into(k, g, dst, sources):
        def total(*index):
            out = dst[index].astype(F32)
            for source in sources:
                out = out + source[index].astype(F32)
            dst[index] = out.astype(BF16)

        if k > 0:
            for b in range(3 if g & 1 else 1):
                total(b)
        else:
            wide = 3 if g & 1 else 1

            def one(n, carry):
                total(lax.div(n, wide), lax.rem(n, wide))
                return carry

            lax.fori_loop(0, BLOCKS[g], one, 0)
        clock.now += 0.03 * BLOCKS[g]

    def rs_start(k, p, g):
        due = [rs_send(k, p, g, n) for n in range(4)]

        def relay():
            taken(rs_r.at[p, slot(k, g), 0], k, p, g, False)
            last = []
            for n in range(2):
                add_into(k, g, region(ps, p, n, k, g, (1, 3)[n]), (rs_place(k, p, g, n),))
                last.append(rs_send(k, p, g, n + 4))
            clock.later(max(due + last), (("fwd", p, 0),), finish)
            if k == 0:
                for follower in {3: (2, 1), 2: (0,)}.get(g, ()):
                    rs_start(0, p, follower)

        def finish():
            taken(rs_r.at[p, slot(k, g), 1], k, p, g, True)
            for h in range(2):
                places = [rs_place(k, p, g, m) for m in range(2, 6) if HALVES[m] == h]
                add_into(k, g, region(ps, p, h, k, g, 0), places)
            done = clock.done
            done.add(("rs", k, p, g))
            if k == 0 and g & 2:
                rs_start(1, p, g & 1)
            if (k, g) in ((0, 1), (1, 1)) and done.issuperset((("rs", 0, p, 1), ("rs", 1, p, 1))):
                rs_start(2, p, 0)
            if done.issuperset(("rs", m, p, 0) for m in range(3)):
                for h in range(2):
                    mst[64 * h:64 * h + 64, 256 * p:256 * (p + 1)] = ps[p, h, 0, 0, 0]
                done.add(("sum", p))

        clock.later(max(due[:2]), (), relay)

    own = go.at[:, :, 0, 0, 0]
    pltpu.make_async_copy(own, own, gl).wait()
    def info_copy(axis, n):
        q, side = ((3, 1), (1, -1), (2, 2))[n]
        src, dst = (info.at[0, 0], info.at[0, q]) if axis == "y" else (info.at[0], info.at[q])
        i = ("y", "z").index(axis) * 3 + n
        return remote(src, dst, in_s.at[i], in_r.at[i], near(axis, side))

    def info_start(axis):
        due = [clock.send(info_copy(axis, n), 0.1, (axis, (1, -1, 1)[n])) for n in range(3)]

        def finish():
            for n in range(3):
                info_copy(axis, n).wait_recv()
            clock.done.add(("info", axis))
            if axis == "y":
                info_start("z")

        clock.later(max(due) + 1.0, (), finish)

    info_start("y")
    for k in (2, 1, 0):
        for p in range(3):
            ag_start(k, p, 0)

    def h_copy(e, device):
        return remote(hid, hv.at[:, pl.ds(pl.multiple_of(e * 64, 64), 64), :], h_s, h_r, device)

    def w_copy(b, e, of, device):
        cols = pl.ds(pl.multiple_of(b * 1536 + of * 768, 128), 768)
        rows = pl.ds(pl.multiple_of(e * 512, 512), 512)
        return remote(w.at[:, cols], wv.at[rows, pl.ds(b * 768, 768)], w_s, w_r, device)

    h_copy(c, partner).start()
    for b in range(4):
        w_copy(b, c, oc, partner).start()

    def turning(e):
        def turn(n, carry):
            pair = jnp.concatenate([hv[n * 2, e * 64:e * 64 + 64, :], hv[n * 2 + 1, e * 64:e * 64 + 64, :]], axis=0)
            ht[e, :, pl.ds(pl.multiple_of(n * 128, 128), 128)] = pair.T
            return carry

        lax.fori_loop(0, 8, turn, 0)

    place = lax.broadcasted_iota(jnp.int32, (128, 128), 0).astype(F32)
    lane = lax.broadcasted_iota(jnp.int32, (128, 128), 1)

    def mix(d, carry):
        zz, yy = lax.div(d, 4), lax.rem(d, 4)
        part = info[rel("z", zz), rel("y", yy)]
        first = jnp.where(part[0:1, :] == place, part[2:3, :], 0.0)
        second = jnp.where(part[1:2, :] == place - 64.0, part[3:4, :], 0.0)
        spread = first + second
        gm[d] = spread.astype(BF16)
        turned = spread.T
        rows = hv[d]
        mv[zz, yy, :, 0:512] = dot(jnp.where(lane < 64, turned, 0.0).astype(BF16), rows).astype(BF16)
        mv[zz, yy, :, 512:1024] = dot(jnp.where(lane < 64, 0.0, turned).astype(BF16), rows).astype(BF16)
        return carry

    def mixing(m):
        lax.fori_loop(4 * m, 4 * m + 4, mix, 0)

    def forward(p, j):
        chunk_at = at(AXES[p][0], j)

        def tile(n, carry):
            if p == 0:
                left = mv[at("z", n)]
                cols = chunk_at * 768
            elif p == 1:
                left = mv[:, chunk_at]
                cols = n * 768 + 256
            else:
                left = mv[chunk_at]
                cols = n * 768 + 512
            right = wv[:, pl.ds(pl.multiple_of(cols, 128), 256)]
            out = dot(left.reshape(512, 1024), right).astype(BF16)
            for q in range(4):
                for h in range(2):
                    piece = out[128 * q + 64 * h:128 * q + 64 * h + 64]
                    if p == 0:
                        ps[p, h, j, rel("y", q), n] = piece
                    elif p == 1:
                        ps[p, h, j, rel("z", q), rel("x", n)] = piece
                    else:
                        ps[p, h, j, rel("x", n), rel("y", q)] = piece
            return carry

        lax.fori_loop(0, 4, tile, 0)
        clock.done.add(("fwd", p, j))

    def gw_out(b, mine):
        e = c if mine else oc
        cols = pl.ds(pl.multiple_of(b * 1536 + c * 768, 128), 768)
        if mine:
            return pltpu.make_async_copy(gws.at[e], gwt.at[:, cols], gwl)
        return remote(gws.at[e], gwt.at[:, cols], gw_s, gw_r, partner)

    def routed(b):
        def one(d, carry):
            zz, yy = lax.div(d, 4), lax.rem(d, 4)
            left = gm[d]
            start = pl.multiple_of(d * 64, 64)
            rx, ry, rz = rel("x", b), rel("y", yy), rel("z", zz)
            for p, (i, j, k) in enumerate(((rx, ry, rz), (ry, rz, rx), (rz, rx, ry))):
                right = jnp.concatenate([go[p, 0, i, j, k], go[p, 1, i, j, k]], axis=0)
                out = dot(left, right).astype(BF16)
                rv[0, pl.ds(start, 64), 256 * p:256 * (p + 1)] = out[0:64]
                rv[1, pl.ds(start, 64), 256 * p:256 * (p + 1)] = out[64:128]
            return carry

        lax.fori_loop(0, 16, one, 0)

    def weight_grad(b, mine):
        e = c if mine else oc
        if b:
            if mine:
                gw_out(b - 1, True).wait()
            else:
                gw_out(b - 1, False).wait_send()

        def one(n, carry):
            cols = pl.ds(pl.multiple_of(n * 256, 256), 256)
            gws[e, :, cols] = dot(ht[e], rv[e, :, cols]).astype(BF16)
            return carry

        lax.fori_loop(0, 3, one, 0)
        gw_out(b, mine).start()

    def hidden_grad(b, e):
        def one(n, carry):
            rows = pl.ds(pl.multiple_of(n * 256, 256), 256)
            right = wv[pl.ds(pl.multiple_of(e * 512, 512), 512), pl.ds(b * 768, 768)]
            out = lax.dot_general(rv[e, rows, :], right, DN_T, preferred_element_type=F32)
            acc[e, rows, :] = out if b == 0 else acc[e, rows, :] + out
            return carry

        lax.fori_loop(0, 4, one, 0)

    h_local.wait()
    h_copy(oc, partner).wait_recv()
    clock.now += 4.0
    clock.run(1.0, turning, 0)
    clock.run(1.0, turning, 1)
    clock.wait([("info", "z")])
    for m in range(4):
        clock.run(0.8, mixing, m)
    mine, theirs = (wv.at[pl.ds(pl.multiple_of(e * 512, 512), 512)] for e in (c, oc))
    pltpu.make_async_copy(mine, mine, wl).wait()
    remote(theirs, theirs, w_s, w_r, partner).wait_recv()
    for j in (2, 1, 3):
        for p in range(3):
            clock.run(2.2, forward, p, j)
    for p in range(3):
        clock.later(clock.now, [("passed", 0, p, g) for g in range(4)], lambda p=p: rs_start(0, p, 3))
    for p in range(3):
        clock.run(2.2, forward, p, 0)
    clock.wait([("ag", 0, p, g) for p in range(3) for g in range(4)])
    for b in range(4):
        clock.run(2.6, routed, b)
        clock.run(1.8, weight_grad, b, False)
        clock.run(1.8, hidden_grad, b, oc)
        clock.run(1.8, weight_grad, b, True)
        clock.run(1.8, hidden_grad, b, c)

    gh_copy = remote(hv.at[:, 0:64, :], ghr, gh_s, gh_r, partner)

    def pack(d, carry):
        hv[d, 0:64, :] = acc[oc, pl.ds(pl.multiple_of(d * 64, 64), 64), :].astype(BF16)
        return carry

    def close(d, carry):
        own = acc[c, pl.ds(pl.multiple_of(d * 64, 64), 64), :]
        hv[d, 64:128, :] = (own + ghr[d].astype(F32)).astype(BF16)
        return carry

    clock.run(0.5, lax.fori_loop, 0, 16, pack, 0)
    gh_copy.start()
    clock.run(4.0, lambda: None)
    clock.flush()
    gh_copy.wait_recv()
    clock.run(0.5, lax.fori_loop, 0, 16, close, 0)
    gh_out = pltpu.make_async_copy(hv.at[:, 64:128, :], ghid, outl.at[0])
    gh_out.start()
    clock.wait([("sum", p) for p in range(3)])
    mixed_out = pltpu.make_async_copy(mst, mixed, outl.at[1])
    mixed_out.start()

    for k, all_sent in enumerate((go.at[:, :, 0:3], go.at[:, :, 0, 0:3], go.at[:, :, 0, 0, 0:3])):
        for sem in (ag_s.at[k], rs_s.at[k]):
            remote(all_sent, all_sent, sem, sem, partner).wait_send()
    for axis in "yz":
        for n in range(3):
            info_copy(axis, n).wait_send()
    h_copy(c, partner).wait_send()
    remote(mine, mine, w_s, w_r, partner).wait_send()
    landed = gwt.at[:, 0:3072]
    remote(landed, landed, gw_s, gw_r, partner).wait_recv()
    gw_out(3, False).wait_send()
    gw_out(3, True).wait()
    gh_copy.wait_send()
    gh_out.wait()
    mixed_out.wait()


def hand_on(a, b, c, a_out, b_out, c_out, av, bv, cv, isem, osem):
    steps = [(a, av, a_out, None), (b, bv, b_out, None)] + [(c, cv, c_out, n) for n in range(8)]
    copies = []
    for i, (src, mid, dst, n) in enumerate(steps):
        if n is not None:
            rows = pl.ds(64 * n, 64)
            src, mid, dst = src.at[rows], mid.at[rows], dst.at[rows]
        copies.append(
            (pltpu.make_async_copy(src, mid, isem.at[i]), pltpu.make_async_copy(mid, dst, osem.at[i]))
        )
    for first, _ in copies:
        first.start()
    for first, second in copies:
        first.wait()
        second.start()
    for _, second in copies:
        second.wait()


def body(hidden, down_weight, grad_out, routing, gates):
    dma = pltpu.SemaphoreType.DMA
    sums = []
    for lead in ((4, 4), (4,), ()):
        sums += [pltpu.VMEM((3, *(lead or (1,)), 64, 256), BF16)] * 2
        sums += [pltpu.VMEM((3, 2, *(lead or (1,)), 64, 256), BF16)] * 2
    anywhere = pl.BlockSpec(memory_space=pl.ANY)
    inside = pl.BlockSpec(memory_space=pltpu.VMEM)
    outs = (
        jax.ShapeDtypeStruct((128, 768), BF16),
        jax.ShapeDtypeStruct((16, 64, 512), BF16),
        jax.ShapeDtypeStruct((512, 6144), BF16),
    )
    results = pl.pallas_call(
        kernel,
        out_shape=outs,
        in_specs=[anywhere, anywhere, anywhere, inside, inside],
        out_specs=(anywhere, anywhere, anywhere),
        scratch_shapes=[
            pltpu.VMEM((3, 2, 4, 4, 4, 64, 256), BF16),
            pltpu.VMEM((3, 2, 4, 4, 4, 64, 256), BF16),
            *sums,
            pltpu.VMEM((1024, 3072), BF16),
            pltpu.VMEM((16, 128, 512), BF16),
            pltpu.VMEM((2, 512, 1024), BF16),
            pltpu.VMEM((4, 4, 128, 1024), BF16),
            pltpu.VMEM((2, 1024, 768), BF16),
            pltpu.VMEM((2, 1024, 512), F32),
            pltpu.VMEM((2, 512, 768), BF16),
            pltpu.VMEM((16, 64, 512), BF16),
            pltpu.VMEM((16, 128, 128), BF16),
            pltpu.VMEM((4, 4, 8, 128), F32),
            pltpu.VMEM((128, 768), BF16),
            dma((3,)), dma((3, 7, 2)), dma((3,)), dma((3, 7, 2)),
            dma(()), dma(()), dma(()), dma(()), dma((6,)), dma((6,)),
            dma(()), dma(()), dma(()), dma(()),
            dma(()), dma(()), dma(()), dma(()), dma((2,)),
        ],
        compiler_params=pltpu.CompilerParams(
            collective_id=0, has_side_effects=True, vmem_limit_bytes=67043328
        ),
    )(
        hidden.reshape(16, 64, 512),
        down_weight[0],
        grad_out,
        routing.T,
        gates.T,
    )
    mixed, ghid, gwt = pl.pallas_call(
        hand_on,
        out_shape=outs,
        in_specs=[anywhere] * 3,
        out_specs=(anywhere,) * 3,
        scratch_shapes=[pltpu.VMEM(out.shape, BF16) for out in outs] + [dma((10,)), dma((10,))],
        compiler_params=pltpu.CompilerParams(vmem_limit_bytes=67043328),
    )(*results)
    return mixed, ghid.reshape(1, 1024, 512), gwt[None]


def solution(mesh):
    return jax.shard_map(
        body,
        mesh=mesh,
        in_specs=(
            P("expert", None, "dp"),
            P("expert", "dp", None),
            P("dp", "expert"),
            P("dp", None),
            P("dp", None),
        ),
        out_specs=(P("dp", "expert"), P("expert", None, "dp"), P("expert", "dp", None)),
        check_vma=False,
    )
```

```python
import jax
import jax.numpy as jnp
from jax import lax
from jax.experimental import pallas as pl
from jax.experimental.pallas import tpu as pltpu
from jax.sharding import PartitionSpec as P

AXES = (("x", "y", "z"), ("y", "z", "x"), ("z", "x", "y"))
MESH = pl.DeviceIdType.MESH
BF16 = jnp.bfloat16
F32 = jnp.float32
RATE = 1.4
HOP = 2.0
FWD, ROUTED, WEIGHT, HIDDEN = 1.1, 1.3, 0.6, 0.9
DN_T = (((1,), (1,)), ((), ()))


def dot(a, b):
    return jnp.dot(a, b, preferred_element_type=F32)


class Clock:
    def __init__(self):
        self.now, self.links, self.pending, self.done, self.count = 0.0, {}, [], set(), 0
        self.places, self.place = {}, None

    def act(self, what):
        self.places.setdefault(self.place, []).append(what)

    def send(self, copy, size, link):
        self.act(lambda: copy().start())
        begin = max(self.now, self.links.get(link, 0.0))
        self.links[link] = begin + size / RATE
        return self.links[link] + HOP

    def later(self, ready, needs, event):
        self.count += 1
        self.pending.append((ready, self.count, needs, event))

    def step(self, limit):
        able = [item for item in self.pending if item[0] <= limit and self.done.issuperset(item[2])]
        if not able:
            return False
        item = min(able, key=lambda item: item[:2])
        self.pending.remove(item)
        self.now = max(self.now, item[0])
        item[3]()
        return True

    def run(self, place, cost=0.0, tags=()):
        self.place = place
        while self.step(self.now):
            pass
        while not self.done.issuperset(tags):
            assert self.step(float("inf"))
        self.now += cost

    def emit(self, *places, index=None):
        for value, place in enumerate(places):
            todo = self.places.pop(place, ())

            def all_of(todo=todo):
                for what in todo:
                    what()

            if todo and index is not None:
                pl.when(index == value)(all_of)
            elif todo:
                all_of()


def kernel(
    hid, w, gin, rt, gt,
    mixed, ghid, gwt,
    go, ps, rx1, fl1, fr1, rx2, fl2, fr2, rx3, fl3, fr3,
    wv, hv, ht, mv, rv, acc, gws, ghr, gm, info, mst, rv_i, rv_g,
    ag_s, ag_r, rs_s, rs_r, w_s, w_r, h_s, h_r, in_s, in_r, gw_s, gw_r, gh_s, gh_r,
    wl, hl, gl, gwl, outl, rl,
):
    dp = lax.axis_index("dp")
    ex = lax.axis_index("expert")
    z, y = lax.div(dp, 4), lax.rem(dp, 4)
    x, c = lax.div(ex, 2), lax.rem(ex, 2)
    oc = 1 - c
    co = {"x": x, "y": y, "z": z}
    clock = Clock()

    def at(axis, delta):
        return lax.rem(co[axis] + delta, 4)

    def rel(axis, place):
        return lax.rem(place + 4 - co[axis], 4)

    def near(axis, delta):
        q = dict(co)
        q[axis] = at(axis, delta % 4)
        return (q["z"] * 4 + q["y"], q["x"] * 2 + c)

    partner = (dp, x * 2 + oc)

    def remote(src, dst, ssem, rsem, device):
        return pltpu.make_async_remote_copy(
            src_ref=src, dst_ref=dst, send_sem=ssem, recv_sem=rsem, device_id=device, device_id_type=MESH
        )

    barrier = pltpu.get_barrier_semaphore()

    for device in [near(axis, side) for axis in "xyz" for side in (1, -1)] + [near("y", 2), near("z", 2), partner]:
        pl.semaphore_signal(barrier, inc=1, device_id=device, device_id_type=MESH)

    def w_local(b):
        cols = pl.ds(pl.multiple_of(b * 1536 + c * 768, 128), 768)
        rows = pl.ds(pl.multiple_of(c * 512, 512), 512)
        return pltpu.make_async_copy(w.at[:, cols], wv.at[rows, pl.ds(b * 768, 768)], wl)

    def g_local(p, h):
        return pltpu.make_async_copy(
            gin.at[pl.ds(64 * h, 64), pl.ds(256 * p, 256)], go.at[p, h, 0, 0, 0], gl
        )

    h_local = pltpu.make_async_copy(hid, hv.at[:, pl.ds(pl.multiple_of(c * 64, 64), 64), :], hl)
    rt_local = pltpu.make_async_copy(rt, rv_i, rl.at[0])
    gt_local = pltpu.make_async_copy(gt, rv_g, rl.at[1])
    rt_local.start()
    gt_local.start()
    for p in range(3):
        for h in range(2):
            g_local(p, h).start()
    h_local.start()
    for b in range(4):
        w_local(b).start()
    pl.semaphore_wait(barrier, 9)

    def region(ref, p, h, k, g, q):
        one, rest = pl.ds(0, 1), pl.ds(1, 3)
        if k == 2:
            return ref.at[p, h, 0, 0, pl.ds(q, 1) if isinstance(q, int) else q]
        if k == 1:
            return ref.at[p, h, 0, q, rest if g & 1 else one]
        return ref.at[p, h, q, rest if g & 2 else one, rest if g & 1 else one]

    BLOCKS = (1, 3, 3, 9)
    BOTH = pl.ds(0, 2)

    def slot(k, g):
        return (0, 4, 6)[k] + g

    def legs(k, g, way):
        if g:
            return (0, 1, 0), (1, -1, 0), (1, 1, 1), (0, -1, 1), (0, 1, 2), (1, -1, 2)
        side = way if (k, g) in ((0, 1), (1, 0), (2, 0)) else -way
        return (BOTH, side, 0), (BOTH, -side, 1), (BOTH, side, 2)

    def size(g, leg):
        return BLOCKS[g] * (2 if leg[0] is BOTH else 1)

    def taken(ref, k, p, g, late):
        some = region(go, p, BOTH, k, g, pl.ds(1, 2) if late else pl.ds(1, 1))
        remote(some, some, ref, ref, partner).wait_recv()

    def ag_send(k, p, g, leg):
        h, side, stage = leg
        axis, came = AXES[p][k], -side % 4

        def copy():
            src = region(go, p, h, k, g, came if stage == 2 else 0)
            dst = region(go, p, h, k, g, 2 if stage == 2 else came)
            return remote(src, dst, ag_s.at[k], ag_r.at[p, slot(k, g), min(stage, 1)], near(axis, side))

        return clock.send(copy, size(g, leg), (axis, side))

    def ag_start(k, p, g):
        group = legs(k, g, 1)
        due = [(ag_send(k, p, g, leg), leg[2]) for leg in group if leg[2] < 2]

        def relay():
            clock.act(lambda: taken(ag_r.at[p, slot(k, g), 0], k, p, g, False))
            last = [ag_send(k, p, g, leg) for leg in group if leg[2] == 2]
            clock.done.add(("passed", k, p, g))
            clock.later(max([ready for ready, _ in due] + last), (), finish)

        def finish():
            clock.act(lambda: taken(ag_r.at[p, slot(k, g), 1], k, p, g, True))
            clock.done.add(("ag", k, p, g))
            if (k, g) == (2, 0):
                ag_start(1, p, 1)
                ag_start(0, p, 1)
            elif k == 1:
                ag_start(0, p, 2 + g)

        clock.later(max(ready for ready, stage in due if stage == 0), (), relay)

    def rs_place(k, p, g, h, side, stage):
        one, rest = pl.ds(0, 1), pl.ds(1, 3)
        a, b = (rest if g & 2 else one), (rest if g & 1 else one)
        ref = ((rx1, rx2, rx3) if stage == 0 else (fl1, fl2, fl3) if side > 0 else (fr1, fr2, fr3))[k]
        return ref.at[p, h, a, b] if k == 0 else ref.at[p, h, b] if k == 1 else ref.at[p, h]

    def rs_send(k, p, g, leg):
        h, side, stage = leg

        def copy():
            src = region(ps, p, h, k, g, 2 if stage == 0 else side % 4)
            dst = rs_place(k, p, g, h, side, stage)
            return remote(src, dst, rs_s.at[k], rs_r.at[p, slot(k, g), min(stage, 1)], near(AXES[p][k], side))

        return clock.send(copy, size(g, leg), (AXES[p][k], side))

    def add_into(k, p, g, q, h, sources):
        wide = 3 if g & 1 else 1
        dst = region(ps, p, h, k, g, q)
        refs = [rs_place(k, p, g, h, side, stage) for side, stage in sources]

        def one(n, carry):
            index = (lax.div(n, wide), lax.rem(n, wide)) if k == 0 else (n,)
            total = dst[index].astype(F32)
            for ref in refs:
                total = total + ref[index].astype(F32)
            dst[index] = total.astype(BF16)
            return carry

        lax.fori_loop(0, BLOCKS[g], one, 0)

    def rs_start(k, p, g):
        group = legs(k, g, -1)
        due = [(rs_send(k, p, g, leg), leg[2]) for leg in group if leg[2] < 2]

        def relay():
            clock.act(lambda: taken(rs_r.at[p, slot(k, g), 0], k, p, g, False))
            last = []
            for leg in group:
                if leg[2] < 2:
                    continue
                for h in (0, 1) if leg[0] is BOTH else (leg[0],):
                    clock.act(lambda h=h, side=leg[1]: add_into(k, p, g, side % 4, h, ((side, 0),)))
                    clock.now += 0.03 * BLOCKS[g]
                last.append(rs_send(k, p, g, leg))
            clock.later(max([ready for ready, _ in due] + last), (("fwd", p, 0),), finish)
            if k == 0:
                for follower in {3: (2, 1), 2: (0,)}.get(g, ()):
                    rs_start(0, p, follower)

        def finish():
            clock.act(lambda: taken(rs_r.at[p, slot(k, g), 1], k, p, g, True))
            for h in range(2):
                clock.act(lambda h=h: add_into(k, p, g, 0, h, ((1, 1), (-1, 1))))
                clock.now += 0.03 * BLOCKS[g]
            done = clock.done
            done.add(("rs", k, p, g))
            if k == 0 and g & 2:
                rs_start(1, p, g & 1)
            if (k, g) in ((0, 1), (1, 1)) and done.issuperset((("rs", 0, p, 1), ("rs", 1, p, 1))):
                rs_start(2, p, 0)
            if done.issuperset(("rs", m, p, 0) for m in range(3)):
                def set_down():
                    for h in range(2):
                        mst[64 * h:64 * h + 64, 256 * p:256 * (p + 1)] = ps[p, h, 0, 0, 0]

                clock.act(set_down)
                done.add(("sum", p))

        clock.later(max(ready for ready, stage in due if stage == 0), (), relay)

    own = go.at[:, :, 0, 0, 0]
    pltpu.make_async_copy(own, own, gl).wait()
    clock.run("first")
    for p in range(3):
        ag_start(2, p, 0)
    clock.emit("first")
    def info_copy(axis, n):
        q, side = ((3, 1), (1, -1), (2, 2))[n]
        src, dst = (info.at[0, 0], info.at[0, q]) if axis == "y" else (info.at[0], info.at[q])
        i = ("y", "z").index(axis) * 3 + n
        return remote(src, dst, in_s.at[i], in_r.at[i], near(axis, side))

    def info_start(axis):
        due = [clock.send(lambda n=n: info_copy(axis, n), 0.1, (axis, (1, -1, 1)[n])) for n in range(3)]

        def finish():
            def all_in():
                for n in range(3):
                    info_copy(axis, n).wait_recv()

            clock.act(all_in)
            clock.done.add(("info", axis))
            if axis == "y":
                info_start("z")

        clock.later(max(due) + 1.0, (), finish)

    rt_local.wait()
    gt_local.wait()
    row = lax.broadcasted_iota(jnp.int32, (8, 128), 0)
    eid = x * 2 + lax.rem(row, 2)
    is0 = rv_i[0:1, :] == eid
    is1 = rv_i[1:2, :] == eid
    gate = jnp.where(is0, rv_g[0:1, :], 0.0) + jnp.where(is1, rv_g[1:2, :], 0.0)
    named = jnp.where(is0, 1.0, 0.0) + jnp.where(is1, 1.0, 0.0)
    before = jnp.where(
        lax.broadcasted_iota(jnp.int32, (128, 128), 0) < lax.broadcasted_iota(jnp.int32, (128, 128), 1), 1.0, 0.0
    )
    rank = dot(jnp.concatenate([named, named], axis=0).astype(BF16), before.astype(BF16))[0:8, :]
    info[0, 0] = jnp.where(row < 2, jnp.where(named > 0.5, rank, -1.0), gate)

    clock.run("second")
    info_start("y")
    for k in (1, 0):
        for p in range(3):
            ag_start(k, p, 0)
    clock.emit("second")

    def h_copy(e, device):
        return remote(hid, hv.at[:, pl.ds(pl.multiple_of(e * 64, 64), 64), :], h_s, h_r, device)

    def w_copy(b, e, of, device):
        cols = pl.ds(pl.multiple_of(b * 1536 + of * 768, 128), 768)
        rows = pl.ds(pl.multiple_of(e * 512, 512), 512)
        return remote(w.at[:, cols], wv.at[rows, pl.ds(b * 768, 768)], w_s, w_r, device)

    h_copy(c, partner).start()
    for b in range(4):
        w_copy(b, c, oc, partner).start()

    def turning(e):
        def turn(n, carry):
            pair = jnp.concatenate([hv[n * 2, e * 64:e * 64 + 64, :], hv[n * 2 + 1, e * 64:e * 64 + 64, :]], axis=0)
            ht[e, :, pl.ds(pl.multiple_of(n * 128, 128), 128)] = pair.T
            return carry

        lax.fori_loop(0, 8, turn, 0)

    place = lax.broadcasted_iota(jnp.int32, (128, 128), 0).astype(F32)
    lane = lax.broadcasted_iota(jnp.int32, (128, 128), 1)

    def mix(d, carry):
        zz, yy = lax.div(d, 4), lax.rem(d, 4)
        part = info[rel("z", zz), rel("y", yy)]
        first = jnp.where(part[0:1, :] == place, part[2:3, :], 0.0)
        second = jnp.where(part[1:2, :] == place - 64.0, part[3:4, :], 0.0)
        spread = first + second
        gm[d] = spread.astype(BF16)
        turned = spread.T
        rows = hv[d]
        mv[zz, yy, :, 0:512] = dot(jnp.where(lane < 64, turned, 0.0).astype(BF16), rows).astype(BF16)
        mv[zz, yy, :, 512:1024] = dot(jnp.where(lane < 64, 0.0, turned).astype(BF16), rows).astype(BF16)
        return carry

    def mixing(m, carry):
        clock.emit(*[("mix", v) for v in range(4)], index=m)
        return lax.fori_loop(4 * m, 4 * m + 4, mix, carry)

    def forward(p):
        def step(s, carry):
            clock.emit(*[("fwd", p, v) for v in range(8)], index=s)
            j = lax.rem(6 - lax.div(s, 2), 4)
            chunk_at = at(AXES[p][0], j)

            def tile(n, carry):
                if p == 0:
                    left = mv[at("z", n)]
                    cols = chunk_at * 768
                elif p == 1:
                    left = mv[:, chunk_at]
                    cols = n * 768 + 256
                else:
                    left = mv[chunk_at]
                    cols = n * 768 + 512
                right = wv[:, pl.ds(pl.multiple_of(cols, 128), 256)]
                out = dot(left.reshape(512, 1024), right).astype(BF16)
                for q in range(4):
                    for h in range(2):
                        piece = out[128 * q + 64 * h:128 * q + 64 * h + 64]
                        if p == 0:
                            ps[p, h, j, rel("y", q), n] = piece
                        elif p == 1:
                            ps[p, h, j, rel("z", q), rel("x", n)] = piece
                        else:
                            ps[p, h, j, rel("x", n), rel("y", q)] = piece
                return carry

            start = 2 * lax.rem(s, 2)
            return lax.fori_loop(start, start + 2, tile, carry)

        lax.fori_loop(0, 8, step, 0)

    def gw_out(b, mine):
        e = c if mine else oc
        cols = pl.ds(pl.multiple_of(b * 1536 + c * 768, 128), 768)
        if mine:
            return pltpu.make_async_copy(gws.at[e], gwt.at[:, cols], gwl)
        return remote(gws.at[e], gwt.at[:, cols], gw_s, gw_r, partner)

    def routed(b):
        def one(d, carry):
            zz, yy = lax.div(d, 4), lax.rem(d, 4)
            left = gm[d]
            start = pl.multiple_of(d * 64, 64)
            rx, ry, rz = rel("x", b), rel("y", yy), rel("z", zz)
            for p, (i, j, k) in enumerate(((rx, ry, rz), (ry, rz, rx), (rz, rx, ry))):
                right = jnp.concatenate([go[p, 0, i, j, k], go[p, 1, i, j, k]], axis=0)
                out = dot(left, right).astype(BF16)
                rv[0, pl.ds(start, 64), 256 * p:256 * (p + 1)] = out[0:64]
                rv[1, pl.ds(start, 64), 256 * p:256 * (p + 1)] = out[64:128]
            return carry

        def some(m, carry):
            clock.emit(*[("routed", v) for v in range(8)], index=2 * b + m)
            return lax.fori_loop(8 * m, 8 * m + 8, one, carry)

        lax.fori_loop(0, 2, some, 0)

    def weight_grad(b):
        def one(i, carry):
            clock.emit(*[("weight", v) for v in range(24)], index=6 * b + i)
            last = b - 1

            @pl.when(jnp.logical_and(b > 0, i == 0))
            def _():
                gw_out(last, False).wait_send()

            @pl.when(jnp.logical_and(b > 0, i == 3))
            def _():
                gw_out(last, True).wait()

            mine = lax.div(i, 3)
            e = mine * c + (1 - mine) * oc
            cols = pl.ds(pl.multiple_of(lax.rem(i, 3) * 256, 256), 256)
            gws[e, :, cols] = dot(ht[e], rv[e, :, cols]).astype(BF16)

            @pl.when(i == 2)
            def _():
                gw_out(b, False).start()

            @pl.when(i == 5)
            def _():
                gw_out(b, True).start()

            return carry

        lax.fori_loop(0, 6, one, 0)

    gh_copy = remote(hv.at[:, 0:64, :], ghr, gh_s, gh_r, partner)

    def pack(d, carry):
        hv[d, 0:64, :] = acc[oc, pl.ds(pl.multiple_of(d * 64, 64), 64), :].astype(BF16)
        return carry

    def close(d, carry):
        own = acc[c, pl.ds(pl.multiple_of(d * 64, 64), 64), :]
        hv[d, 64:128, :] = (own + ghr[d].astype(F32)).astype(BF16)
        return carry

    def hidden_grad(b):
        right_cols = pl.ds(pl.multiple_of(b * 768, 128), 768)

        def some(i, carry):
            clock.emit(*[("hidden", v) for v in range(16)], index=4 * b + i)

            @pl.when(jnp.logical_and(b == 3, i == 2))
            def _():
                lax.fori_loop(0, 16, pack, 0)
                gh_copy.start()

            mine = lax.div(i, 2)
            e = mine * c + (1 - mine) * oc

            def one(n, carry):
                rows = pl.ds(pl.multiple_of(n * 256, 256), 256)
                right = wv[pl.ds(pl.multiple_of(e * 512, 512), 512), right_cols]
                out = lax.dot_general(rv[e, rows, :], right, DN_T, preferred_element_type=F32)
                acc[e, rows, :] = acc[e, rows, :] + out
                return carry

            start = 2 * lax.rem(i, 2)
            return lax.fori_loop(start, start + 2, one, carry)

        lax.fori_loop(0, 4, some, 0)

    def backward(b, carry):
        routed(b)
        hidden_grad(b)
        weight_grad(b)
        return carry

    def clear(n, carry):
        rows = pl.ds(pl.multiple_of(n * 64, 64), 64)
        for e in range(2):
            acc[e, rows, :] = jnp.zeros((64, 512), F32)
        return carry

    clock.now += 4.0
    clock.run("turn", 2.0)
    clock.run("info", 0.0, [("info", "z")])
    for m in range(4):
        clock.run(("mix", m), 0.75)
    for p in range(3):
        for v in range(8):
            clock.run(("fwd", p, v), FWD)
        clock.done.add(("fwd", p, 0))
        clock.later(clock.now, [("passed", 0, p, g) for g in range(4)], lambda p=p: rs_start(0, p, 3))
    clock.run("gathered", 0.0, [("ag", 0, p, g) for p in range(3) for g in range(4)])
    for b in range(4):
        for m in range(2):
            clock.run(("routed", 2 * b + m), ROUTED)
        for i in range(4):
            clock.run(("hidden", 4 * b + i), HIDDEN)
        for i in range(6):
            clock.run(("weight", 6 * b + i), WEIGHT)
    clock.run("close", 0.5)
    clock.run("summed", 0.0, [("sum", p) for p in range(3)])

    h_local.wait()
    h_copy(oc, partner).wait_recv()
    clock.emit("turn")
    lax.fori_loop(0, 16, clear, 0)
    turning(0)
    turning(1)
    clock.emit("info")
    lax.fori_loop(0, 4, mixing, 0)
    mine, theirs = (wv.at[pl.ds(pl.multiple_of(e * 512, 512), 512)] for e in (c, oc))
    pltpu.make_async_copy(mine, mine, wl).wait()
    remote(theirs, theirs, w_s, w_r, partner).wait_recv()
    for p in range(3):
        forward(p)
    clock.emit("gathered")
    lax.fori_loop(0, 4, backward, 0)
    clock.emit("close")
    gh_copy.wait_recv()
    lax.fori_loop(0, 16, close, 0)
    gh_out = pltpu.make_async_copy(hv.at[:, 64:128, :], ghid, outl.at[0])
    gh_out.start()
    clock.emit("summed")
    assert not clock.places and not clock.pending
    mixed_out = pltpu.make_async_copy(mst, mixed, outl.at[1])
    mixed_out.start()

    for k, all_sent in enumerate((go.at[:, :, 0:3], go.at[:, :, 0, 0:3], go.at[:, :, 0, 0, 0:3])):
        for sem in (ag_s.at[k], rs_s.at[k]):
            remote(all_sent, all_sent, sem, sem, partner).wait_send()
    for axis in "yz":
        for n in range(3):
            info_copy(axis, n).wait_send()
    h_copy(c, partner).wait_send()
    remote(mine, mine, w_s, w_r, partner).wait_send()
    landed = gwt.at[:, 0:3072]
    remote(landed, landed, gw_s, gw_r, partner).wait_recv()
    gw_out(3, False).wait_send()
    gw_out(3, True).wait()
    gh_copy.wait_send()
    gh_out.wait()
    mixed_out.wait()


def hand_on(a, b, c, a_out, b_out, c_out, av, bv, cv, isem, osem):
    steps = [(a, av, a_out, None), (b, bv, b_out, None)] + [(c, cv, c_out, n) for n in range(8)]
    copies = []
    for i, (src, mid, dst, n) in enumerate(steps):
        if n is not None:
            rows = pl.ds(64 * n, 64)
            src, mid, dst = src.at[rows], mid.at[rows], dst.at[rows]
        copies.append(
            (pltpu.make_async_copy(src, mid, isem.at[i]), pltpu.make_async_copy(mid, dst, osem.at[i]))
        )
    for first, _ in copies:
        first.start()
    for first, second in copies:
        first.wait()
        second.start()
    for _, second in copies:
        second.wait()


def body(hidden, down_weight, grad_out, routing, gates):
    dma = pltpu.SemaphoreType.DMA
    sums = []
    for lead in ((4, 4), (4,), ()):
        sums += [pltpu.VMEM((3, 2, *(lead or (1,)), 64, 256), BF16)] * 3
    anywhere = pl.BlockSpec(memory_space=pl.ANY)
    outs = (
        jax.ShapeDtypeStruct((128, 768), BF16),
        jax.ShapeDtypeStruct((16, 64, 512), BF16),
        jax.ShapeDtypeStruct((512, 6144), BF16),
    )
    results = pl.pallas_call(
        kernel,
        out_shape=outs,
        in_specs=[anywhere] * 5,
        out_specs=(anywhere, anywhere, anywhere),
        scratch_shapes=[
            pltpu.VMEM((3, 2, 4, 4, 4, 64, 256), BF16),
            pltpu.VMEM((3, 2, 4, 4, 4, 64, 256), BF16),
            *sums,
            pltpu.VMEM((1024, 3072), BF16),
            pltpu.VMEM((16, 128, 512), BF16),
            pltpu.VMEM((2, 512, 1024), BF16),
            pltpu.VMEM((4, 4, 128, 1024), BF16),
            pltpu.VMEM((2, 1024, 768), BF16),
            pltpu.VMEM((2, 1024, 512), F32),
            pltpu.VMEM((2, 512, 768), BF16),
            pltpu.VMEM((16, 64, 512), BF16),
            pltpu.VMEM((16, 128, 128), BF16),
            pltpu.VMEM((4, 4, 8, 128), F32),
            pltpu.VMEM((128, 768), BF16),
            pltpu.VMEM((2, 128), jnp.int32),
            pltpu.VMEM((2, 128), F32),
            dma((3,)), dma((3, 7, 2)), dma((3,)), dma((3, 7, 2)),
            dma(()), dma(()), dma(()), dma(()), dma((6,)), dma((6,)),
            dma(()), dma(()), dma(()), dma(()),
            dma(()), dma(()), dma(()), dma(()), dma((2,)), dma((2,)),
        ],
        compiler_params=pltpu.CompilerParams(
            collective_id=0, has_side_effects=True, vmem_limit_bytes=67043328
        ),
    )(
        hidden.reshape(16, 64, 512),
        down_weight[0],
        grad_out,
        routing.T,
        gates.T,
    )
    mixed, ghid, gwt = pl.pallas_call(
        hand_on,
        out_shape=outs,
        in_specs=[anywhere] * 3,
        out_specs=(anywhere,) * 3,
        scratch_shapes=[pltpu.VMEM(out.shape, BF16) for out in outs] + [dma((10,)), dma((10,))],
        compiler_params=pltpu.CompilerParams(vmem_limit_bytes=67043328),
    )(*results)
    return mixed, ghid.reshape(1, 1024, 512), gwt[None]


def solution(mesh):
    return jax.shard_map(
        body,
        mesh=mesh,
        in_specs=(
            P("expert", None, "dp"),
            P("expert", "dp", None),
            P("dp", "expert"),
            P("dp", None),
            P("dp", None),
        ),
        out_specs=(P("dp", "expert"), P("expert", None, "dp"), P("expert", "dp", None)),
        check_vma=False,
    )
```
